32 devices in a mesh: fsdp: 16 (over z, y, x), tp: 2 (over core).
Axes of the slice: x: 2, y: 2, z: 4, core: 2. Of those that a mesh axis runs over, the one named last changes fastest.
Arguments:
- tokens: bfloat16 [4096, 896], P(('fsdp', 'tp')), may hold values from -6 to 6
- cotangent: bfloat16 [4096, 896], P(('fsdp', 'tp')), may hold values from -6 to 6
- parents: int32 [16, 2], P('fsdp'), may hold values from 0 to 0, as said below
- skip: int32 [16], P('fsdp'), may hold values 0 or 1
- w_query: bfloat16 [896, 896], P('fsdp', 'tp'), may hold values from -0.1875 to 0.1875
- key_matrix: bfloat16 [896, 128], P('fsdp', 'tp'), may hold values from -0.1875 to 0.1875
- value_matrix: bfloat16 [896, 128], P('fsdp', 'tp'), may hold values from -0.1875 to 0.1875
- w_out: bfloat16 [896, 896], P('tp', 'fsdp'), may hold values from -0.75 to 0.75
- w_gate: bfloat16 [896, 4864], P('fsdp', 'tp'), may hold values from -0.1875 to 0.1875
- w_up: bfloat16 [896, 4864], P('fsdp', 'tp'), may hold values from -0.1875 to 0.1875
- w_down: bfloat16 [4864, 896], P('tp', 'fsdp'), may hold values from -0.078125 to 0.078125
- gain_attn: bfloat16 [896], P('fsdp'), may hold values from 0.5 to 1.5
- gain_mlp: bfloat16 [896], P('fsdp'), may hold values from 0.5 to 1.5
Outputs:
- output: bfloat16 [4096, 896], P(('fsdp', 'tp'))
- grad_tokens: bfloat16 [4096, 896], P(('fsdp', 'tp'))
- grad_w_query: float32 [896, 896], P('fsdp', 'tp')
- grad_w_key: float32 [896, 128], P('fsdp', 'tp')
- grad_w_value: float32 [896, 128], P('fsdp', 'tp')
- grad_w_out: float32 [896, 896], P('tp', 'fsdp')
- grad_w_gate: float32 [896, 4864], P('fsdp', 'tp')
- grad_w_up: float32 [896, 4864], P('fsdp', 'tp')
- grad_w_down: float32 [4864, 896], P('tp', 'fsdp')
- grad_gain_attn: float32 [896], P('fsdp')
- grad_gain_mlp: float32 [896], P('fsdp')
The draws below stay inside these ranges and needn't reach their ends.
Inputs may be any that keep to these rules, and one draw needn't show every extreme that they name: `parents`: block 0 of a tree is its own parent; each tree has two blocks, and block 1 has block 0 as its parent, so every tree's mask is causal and pos is the token's place in its tree.
All inputs are finite; a program needn't handle non-finite values. No bound on the sum of `skip` on one device may be relied on, other than what follows from the above.
Results may differ from the reference program's by a relative error of at most 0.015.
Values may be sent and summed in bfloat16 or wider, within the bound.
No kernel may reach another device: no remote copies, remote signals or barrier semaphores. Data moves between devices by JAX's collectives and lax.ppermute only.
A program may use at most 192 MiB of HBM per device.

```python
import jax
import jax.numpy as jnp
from jax import lax

MODEL_WIDTH = 896
QUERY_HEADS = 14
KEY_VALUE_HEADS = 2
HEAD_SIZE = 64
FF = 4864
BLK = 128
SEQ = 256
TREES = 16
TOKENS = 4096


def draw_parents(key, part):
    blocks = SEQ // BLK
    trunk_blocks = max(1, blocks // 3)
    block_index = jnp.arange(blocks, dtype=jnp.int32)
    lower_end = jnp.maximum(jnp.minimum(block_index - 1, trunk_blocks - 1), 0)
    upper_end = jnp.maximum(block_index - 1, 0)
    random_picks = jax.random.randint(key, (TREES, blocks), 0, 1 << 20, dtype=jnp.int32)
    parent = lower_end[None, :] + random_picks % (upper_end - lower_end + 1)[None, :]
    return jnp.where(block_index[None, :] == blocks - 1, blocks - 2, parent).astype(jnp.int32)


def with_ends(drawn, rng, smallest, top_value):
    longest = drawn.shape.index(max(drawn.shape))
    spots = []
    for shift in (0, 1):
        where = [jax.random.randint(jax.random.fold_in(rng, axis), (), 0, length) for axis, length in enumerate(drawn.shape)]
        where[longest] = (where[longest] + shift) % drawn.shape[longest]
        spots.append(tuple(where))
    return drawn.at[spots[0]].set(smallest).at[spots[1]].set(top_value)


def strengthened(drawn, key, source, target, parts, factor):
    owner, partner = [(jnp.arange(drawn.shape[position]) // (drawn.shape[position] // parts)).reshape([-1 if axis == position else 1 for axis in range(drawn.ndim)]) for position in (source, target)]
    chosen = jax.random.permutation(key, parts)[partner]
    strong = (owner == chosen) | (owner == (partner + parts // 2) % parts)
    return jnp.where(strong, factor * drawn, drawn)


def steps_of(rng, dims, pieces, smallest, high):
    def one(position, blocks):
        steps = jax.random.uniform(jax.random.fold_in(jax.random.fold_in(rng, 6), position), (blocks,), jnp.float32, smallest / len(pieces), high / len(pieces))
        return jnp.repeat(jnp.exp(steps), dims[position] // blocks).reshape((-1,) + (1,) * (len(dims) - position - 1))

    loudness = one(*pieces[0])
    for cut in pieces[1:]:
        loudness = loudness * one(*cut)
    return loudness


def normal_values(stream_key, shape, width, limit, split=(), held_as=jnp.bfloat16):
    loudness = steps_of(stream_key, shape, split, -0.22, 0.18) if split else 1.0
    entries = jax.random.normal(stream_key, shape, jnp.float32) * width * loudness
    return jnp.minimum(jnp.maximum(entries, -limit), limit).astype(held_as)


def heavy_noise(key, extent, width, most, pieces, heavy, kind=jnp.bfloat16):
    values = width * jax.random.normal(key, extent, jnp.float32)
    if pieces:
        values = values * steps_of(key, extent, pieces, -0.22, 0.18)
    return jnp.clip(strengthened(values, jax.random.fold_in(key, 3), *heavy), -most, most).astype(kind)


def setup_inputs(seed: int = 0) -> dict:
    streams_of = jax.random.split(jax.random.key(seed), 14)
    tokens = heavy_noise(streams_of[0], (TOKENS, MODEL_WIDTH), 1.0, 6.0, ((0, 32),), (0, 1, 32, 2.75))
    cotangent = heavy_noise(streams_of[1], (TOKENS, MODEL_WIDTH), 1.0, 6.0, ((0, 32),), (0, 1, 32, 2.75))
    parents = draw_parents(jax.random.fold_in(streams_of[13], 71), 0)
    skip = with_ends((jax.random.randint(streams_of[3], (TREES,), 0, 4) < 1).astype(jnp.int32), jax.random.fold_in(streams_of[3], 1), 0, 1)
    w_query = normal_values(streams_of[4], (MODEL_WIDTH, QUERY_HEADS * HEAD_SIZE), MODEL_WIDTH ** -0.5, 0.1875, ((0, 16), (1, 2)))
    key_matrix = normal_values(streams_of[5], (MODEL_WIDTH, KEY_VALUE_HEADS * HEAD_SIZE), MODEL_WIDTH ** -0.5, 0.1875, ((0, 16), (1, 2)))
    value_matrix = normal_values(streams_of[6], (MODEL_WIDTH, KEY_VALUE_HEADS * HEAD_SIZE), MODEL_WIDTH ** -0.5, 0.1875, ((0, 16), (1, 2)))
    w_out = normal_values(streams_of[7], (QUERY_HEADS * HEAD_SIZE, MODEL_WIDTH), (QUERY_HEADS * HEAD_SIZE // 16) ** -0.5, 0.75, ((0, 2), (1, 16)))
    w_gate = normal_values(streams_of[8], (MODEL_WIDTH, FF), MODEL_WIDTH ** -0.5, 0.1875, ((0, 16), (1, 2)))
    w_up = normal_values(streams_of[9], (MODEL_WIDTH, FF), MODEL_WIDTH ** -0.5, 0.1875, ((0, 16), (1, 2)))
    w_down = normal_values(streams_of[10], (FF, MODEL_WIDTH), FF ** -0.5, 0.078125, ((0, 2), (1, 16)))
    gain_attn = jnp.clip(1.0 + 0.1 * jax.random.normal(streams_of[11], (MODEL_WIDTH,), jnp.float32), 0.5, 1.5).astype(jnp.bfloat16)
    gain_mlp = jnp.clip(1.0 + 0.1 * jax.random.normal(streams_of[12], (MODEL_WIDTH,), jnp.float32), 0.5, 1.5).astype(jnp.bfloat16)
    return {"tokens": tokens, "cotangent": cotangent, "parents": parents, "skip": skip, "w_query": w_query, "key_matrix": key_matrix, "value_matrix": value_matrix, "w_out": w_out, "w_gate": w_gate, "w_up": w_up, "w_down": w_down, "gain_attn": gain_attn, "gain_mlp": gain_mlp}


@jax.custom_vjp
def low(v):
    return lax.optimization_barrier(v.astype(jnp.bfloat16)).astype(jnp.float32)

@jax.custom_vjp
def low_back(v):
    return v

def low_keep(v):
    return (low(v), None)

def low_pass(kept, grad):
    return (grad,)

def back_keep(v):
    return (v, None)

def back_low(kept, grad):
    return (low(grad),)
low.defvjp(low_keep, low_pass)
low_back.defvjp(back_keep, back_low)
eps = 1e-05
rotary_base = 10000.0
highest = lax.Precision.HIGHEST

def tree_tables(parents, blocks, block_len):
    block_ids = jnp.arange(blocks, dtype=jnp.int32)
    ancestry = jnp.eye(blocks, dtype=jnp.float32)
    depths = jnp.zeros((blocks,), jnp.float32)
    for block_number in range(1, blocks):
        picked = (block_ids == parents[block_number]).astype(jnp.float32)
        inherited = lax.optimization_barrier(jnp.sum(picked[:, None] * ancestry, axis=0))
        ancestry = ancestry.at[block_number].set(jnp.maximum(ancestry[block_number], inherited))
        depths = depths.at[block_number].set(jnp.sum(picked * depths) + 1.0)
    token_ids = jnp.arange(blocks * block_len, dtype=jnp.int32)
    spread = jnp.repeat(jnp.repeat(ancestry, block_len, axis=0), block_len, axis=1)
    visible = (spread > 0.5) & (token_ids[None, :] <= token_ids[:, None])
    token_position = jnp.repeat(depths, block_len) * block_len + (token_ids % block_len).astype(jnp.float32)
    return (visible, token_position)

def apply_rotation(values, token_position, head_count, direction):
    count_of_rows = values.shape[0]
    shaped = values.reshape(count_of_rows, head_count, HEAD_SIZE)
    half_size = HEAD_SIZE // 2
    frequency = rotary_base ** (-2.0 * jnp.arange(half_size, dtype=jnp.float32) / HEAD_SIZE)
    angles = token_position[:, None] * frequency[None, :]
    cosine = jnp.cos(angles)[:, None, :]
    sine_part = direction * jnp.sin(angles)[:, None, :]
    first_half = shaped[..., :half_size]
    second_half = shaped[..., half_size:]
    turned = jnp.concatenate([first_half * cosine - second_half * sine_part, second_half * cosine + first_half * sine_part], axis=-1)
    return turned.reshape(count_of_rows, head_count * HEAD_SIZE)

def matrix_product(first_array, second_array):
    return jnp.dot(first_array, second_array, precision=highest, preferred_element_type=jnp.float32)

def normalize(values, gain_vector):
    return values * lax.rsqrt(lax.optimization_barrier(jnp.mean(values * values, axis=-1, keepdims=True)) + eps) * gain_vector

def block_forward(inputs, w_query, key_matrix, value_matrix, w_out, w_gate, w_up, w_down, gain_attn, gain_mlp, active, visible, token_position):
    count_of_rows = inputs.shape[0]
    heads_per_group = QUERY_HEADS // KEY_VALUE_HEADS
    normed_input = low(normalize(inputs, gain_attn))
    query_rows = low(apply_rotation(low_back(matrix_product(normed_input, w_query)), token_position, QUERY_HEADS, 1.0))
    key_row_block = low(apply_rotation(low_back(matrix_product(normed_input, key_matrix)), token_position, KEY_VALUE_HEADS, 1.0))
    value_row_block = low(low_back(matrix_product(normed_input, value_matrix)))
    query_per_head = query_rows.reshape(count_of_rows, KEY_VALUE_HEADS, heads_per_group, HEAD_SIZE)
    key_per_head = key_row_block.reshape(count_of_rows, KEY_VALUE_HEADS, HEAD_SIZE)
    value_per_head = value_row_block.reshape(count_of_rows, KEY_VALUE_HEADS, HEAD_SIZE)
    scores = low_back(jnp.einsum('qhgd,khd->hgqk', query_per_head, key_per_head, precision=highest) * HEAD_SIZE ** (-0.5))
    scores = jnp.where(visible, scores, -1e+30)
    attention = jax.nn.softmax(scores, axis=-1)
    attended = jnp.einsum('hgqk,khd->qhgd', low(attention), value_per_head, precision=highest)
    attended = low(low_back(attended.reshape(count_of_rows, QUERY_HEADS * HEAD_SIZE)))
    branch = low_back(matrix_product(attended, w_out))
    middle = inputs + active * branch
    normed_mlp = low(normalize(middle, gain_mlp))
    gate_sum = low_back(matrix_product(normed_mlp, w_gate))
    upward = low_back(matrix_product(normed_mlp, w_up))
    hidden = low(jax.nn.silu(gate_sum) * upward)
    return middle + active * low_back(matrix_product(hidden, w_down))

def reference(tokens, cotangent, parents, skip, w_query, key_matrix, value_matrix, w_out, w_gate, w_up, w_down, gain_attn, gain_mlp):
    weights = tuple((array.astype(jnp.float32) for array in (w_query, key_matrix, value_matrix, w_out, w_gate, w_up, w_down, gain_attn, gain_mlp)))
    blocks = SEQ // BLK

    def per_tree(totals, element):
        tree_tokens, tree_cot, tree_parents, tree_skip = element
        visible, token_position = tree_tables(tree_parents, blocks, BLK)
        active = (1 - tree_skip).astype(jnp.float32)

        def forward(inputs, *params):
            return block_forward(inputs, *params, active, visible, token_position)
        result, pullback = jax.vjp(forward, tree_tokens.astype(jnp.float32), *weights)
        gradients = pullback(tree_cot.astype(jnp.float32))
        totals = tuple((running + gradient for running, gradient in zip(totals, gradients[1:])))
        return (totals, (result.astype(jnp.bfloat16), gradients[0].astype(jnp.bfloat16)))
    zero_grads = tuple((jnp.zeros(array.shape, jnp.float32) for array in weights))
    sequences = (tokens.reshape(TREES, SEQ, MODEL_WIDTH), cotangent.reshape(TREES, SEQ, MODEL_WIDTH), parents, skip)
    totals, (outputs, token_grads) = lax.scan(per_tree, zero_grads, sequences)
    return (outputs.reshape(TREES * SEQ, MODEL_WIDTH), token_grads.reshape(TREES * SEQ, MODEL_WIDTH), totals[0], totals[1], totals[2], totals[3], totals[4], totals[5], totals[6], totals[7], totals[8])
```

```python
import jax
import jax.numpy as jnp
import numpy as np
from jax import lax
from jax.sharding import Mesh, PartitionSpec as P

HEAD_SIZE = 64
LANES = 128
eps = 1e-05
rotary_base = 10000.0
bf16 = jnp.bfloat16
f32 = jnp.float32
T_AXES = ("z0", "x")
SWAP = [(0, 1), (1, 0)]


def rotary_tables(seq_len, heads):
    half = HEAD_SIZE // 2
    frequency = rotary_base ** (-2.0 * np.arange(half, dtype=np.float32) / HEAD_SIZE)
    angles = np.arange(seq_len, dtype=np.float32)[:, None] * frequency[None, :].astype(np.float32)
    return np.cos(angles).astype(np.float32), np.sin(angles).astype(np.float32)


def rotate(values, cosine, sine):
    rows = values.shape[0]
    half = HEAD_SIZE // 2
    shaped = values.reshape(rows, -1, HEAD_SIZE)
    a = shaped[..., :half]
    b = shaped[..., half:]
    c = cosine[:, None, :]
    s = sine[:, None, :]
    return jnp.concatenate([a * c - b * s, b * c + a * s], axis=-1).reshape(rows, -1)


def nn(a, b):
    return lax.dot_general(a, b, (((1,), (0,)), ((), ())), preferred_element_type=f32)


def tn(a, b):
    return lax.dot_general(a, b, (((0,), (0,)), ((), ())), preferred_element_type=f32)


def nt(a, b):
    return lax.dot_general(a, b, (((1,), (1,)), ((), ())), preferred_element_type=f32)


def swap(value, axis):
    return lax.ppermute(value, axis, SWAP)


def spread(value, axes):
    peers = 1
    for axis in axes:
        peers *= lax.axis_size(axis)
    wide = jnp.broadcast_to(value[None], (peers,) + value.shape)
    return lax.all_to_all(wide, axes, 0, 0, tiled=True)


def t_partner(x_bit, z_bit):
    return [
        (i, (((i // 2) ^ z_bit) * 2) + ((i % 2) ^ x_bit)) for i in range(4)
    ]


def t_send(values):
    return [
        lax.ppermute(v, T_AXES, t_partner(xb, zb))
        for v, (xb, zb) in zip(values, ((1, 0), (0, 1), (1, 1)))
    ]


def share_tokens(own_half):
    got = jnp.stack([own_half] + t_send([own_half] * 3))
    other = swap(got, "tp")
    return jnp.stack([got, other], axis=1)


def return_tokens(partial):
    away = partial[:, 1].astype(bf16)
    mine = (partial[:, 0] + swap(away, "tp").astype(f32)).astype(bf16)
    back = t_send([mine[1], mine[2], mine[3]])
    total = mine[0].astype(f32)
    for b in back:
        total = total + b.astype(f32)
    return total


def gather_g(value):
    if lax.axis_size("z1") == 2:
        first = jnp.stack([value, swap(value, "z1")])
    else:
        first = lax.all_gather(value, "z1", axis=0)
    return jnp.stack([first, swap(first, "y")], axis=1)


def reduce_g(value):
    half = (value[:, 0] + swap(value[:, 1].astype(bf16), "y").astype(f32))
    if lax.axis_size("z1") == 2:
        return half[0] + swap(half[1].astype(bf16), "z1").astype(f32)
    got = lax.all_to_all(half.astype(bf16), "z1", 0, 0, tiled=True)
    return jnp.sum(got.astype(f32), axis=0)


def relative_order(n1, rows):
    width = n1 * 8 * rows
    place = lax.broadcasted_iota(jnp.int32, (1, width), 1)
    row = place % rows
    rest = place // rows
    x = rest % 2
    z0 = (rest // 2) % 2
    y = ((rest // 4) % 2) ^ lax.axis_index("y")
    z1 = rest // 8
    if n1 == 2:
        z1 = z1 ^ lax.axis_index("z1")
    return (((z1 * 2 + z0) * 2 + y) * 2 + x) * rows + row


def on_device(
    tokens, cotangent, parents, skip, w_query, key_matrix, value_matrix, w_out, w_gate, w_up, w_down, gain_attn, gain_mlp
):
    half_rows, width = tokens.shape
    seq_len = 2 * half_rows
    rows = w_query.shape[0]
    n1 = lax.axis_size("z1")
    q_cols = w_query.shape[1]
    kv_cols = key_matrix.shape[1]
    heads = q_cols // HEAD_SIZE
    kv_heads = kv_cols // HEAD_SIZE
    group = heads // kv_heads
    ff = w_gate.shape[1]
    hs = -(-ff // (4 * LANES)) * LANES
    scale = HEAD_SIZE ** (-0.5)
    core = lax.axis_index("tp")
    active = (1 - skip[0]).astype(f32)
    cos_np, sin_np = rotary_tables(seq_len, heads)
    cosine, sine = jnp.asarray(cos_np), jnp.asarray(sin_np)
    visible = np.tril(np.ones((seq_len, seq_len), bool))

    gain_one = gain_attn.astype(f32)[:, None]
    gain_two = gain_mlp.astype(f32)[:, None]

    scaled_w = lambda w, g: (w.astype(f32) * g).astype(bf16)
    attn_w = jnp.concatenate(
        [scaled_w(w_query, gain_one), scaled_w(key_matrix, gain_one), scaled_w(value_matrix, gain_one), w_out.T], axis=1
    )
    along_z = spread(attn_w, ("z1", "z0"))
    everywhere = spread(along_z, ("y", "x"))
    attn_all = everywhere.transpose(1, 0, 2, 3).reshape(width, attn_w.shape[1])
    qkv_w = attn_all[:, : q_cols + 2 * kv_cols]
    out_t = attn_all[:, q_cols + 2 * kv_cols :]

    pad = lambda w: jnp.pad(w, ((0, 0), (0, 4 * hs - ff))).reshape(rows, 4, hs).transpose(1, 0, 2)
    gate_up = jnp.concatenate([pad(scaled_w(w_gate, gain_two)), pad(scaled_w(w_up, gain_two))], axis=2)
    down = pad(w_down.T)
    gu_t = lax.all_to_all(gate_up, T_AXES, 0, 0, tiled=True).reshape(4 * rows, 2 * hs)
    down_t = lax.all_to_all(down, T_AXES, 0, 0, tiled=True).reshape(4 * rows, hs)
    gu_all = gather_g(gu_t).reshape(width, 2 * hs)
    down_all = gather_g(down_t).reshape(width, hs)
    order = relative_order(n1, rows)
    natural = lax.broadcasted_iota(jnp.int32, (width, 1), 0)
    to_relative = (natural == order).astype(bf16)

    other_tokens, other_cot = swap(tokens, "tp"), swap(cotangent, "tp")
    both = lambda mine, other: jnp.where(core == 0, jnp.stack([mine, other]), jnp.stack([other, mine])).reshape(seq_len, width)
    inputs = both(tokens, other_tokens).astype(f32)
    grad_out = both(cotangent, other_cot).astype(f32)
    my_half = lambda v: lax.dynamic_slice_in_dim(v, core * half_rows, half_rows, axis=0)

    grad_mlp = (active * cotangent.astype(f32)).astype(bf16)
    cot_all = share_tokens(nn(grad_mlp, to_relative).astype(bf16)).reshape(8 * half_rows, width)

    stat_one = lax.rsqrt(jnp.mean(inputs * inputs, axis=-1, keepdims=True) + eps)
    scaled_one = inputs * stat_one
    normed = scaled_one.astype(bf16)
    qkv = nn(normed, qkv_w)
    query = rotate(qkv[:, :q_cols], cosine, sine).astype(bf16)
    key = rotate(qkv[:, q_cols : q_cols + kv_cols], cosine, sine).astype(bf16)
    value = qkv[:, q_cols + kv_cols :].astype(bf16)
    q4 = query.reshape(seq_len, kv_heads, group, HEAD_SIZE)
    k3 = key.reshape(seq_len, kv_heads, HEAD_SIZE)
    v3 = value.reshape(seq_len, kv_heads, HEAD_SIZE)
    raw = jnp.einsum("qhgd,khd->hgqk", q4, k3, preferred_element_type=f32) * scale
    scores = jnp.where(visible, raw, -1e30)
    row_max = jnp.max(scores, axis=-1, keepdims=True)
    exponent = jnp.exp(scores - row_max)
    probs = exponent / jnp.sum(exponent, axis=-1, keepdims=True)
    probs_low = probs.astype(bf16)
    attended = jnp.einsum("hgqk,khd->qhgd", probs_low, v3, preferred_element_type=f32)
    attended = attended.reshape(seq_len, q_cols).astype(bf16)
    branch_part = nt(attended, out_t)
    branch = branch_part + swap(branch_part.astype(bf16), "tp").astype(f32)
    branch = branch_part.astype(bf16).astype(f32) + (branch - branch_part)
    middle = inputs + active * branch
    stat_two = lax.rsqrt(jnp.mean(middle * middle, axis=-1, keepdims=True) + eps)
    scaled_two = middle * stat_two
    x_all = share_tokens(nn(my_half(scaled_two).astype(bf16), to_relative).astype(bf16)).reshape(8 * half_rows, width)

    gu = nn(x_all, gu_all)
    gate, up = gu[:, :hs], gu[:, hs:]
    sig = jax.nn.sigmoid(gate)
    hidden = (gate * sig * up).astype(bf16)
    d_hidden = nt(cot_all, down_all.T) if False else nn(cot_all, down_all)
    d_gate = (d_hidden * up * sig * (1.0 + gate * (1.0 - sig))).astype(bf16)
    d_up = (d_hidden * gate * sig).astype(bf16)
    d_gu = jnp.concatenate([d_gate, d_up], axis=1)
    e_part = nt(d_gu, gu_all).reshape(4, 2, half_rows, width)
    e_rel = return_tokens(e_part).astype(bf16)
    e_mine = nt(e_rel, to_relative).astype(bf16)
    grad_down_rel = tn(cot_all, hidden)
    grad_gu_rel = tn(x_all, d_gu)
    mlp_part = nt(hidden, down_all).reshape(4, 2, half_rows, width)
    mlp_mine = nt(return_tokens(mlp_part).astype(bf16), to_relative)
    output = (my_half(middle) + active * mlp_mine).astype(bf16)

    def to_owner(grad):
        cols = grad.shape[1]
        summed = reduce_g(grad.reshape(n1, 2, 4 * rows, cols)).astype(bf16).reshape(4, rows, cols)
        return lax.all_to_all(summed, T_AXES, 0, 0, tiled=True)

    got_down = to_owner(grad_down_rel)
    got_gu = to_owner(grad_gu_rel)
    join = lambda v: v.transpose(1, 0, 2).reshape(rows, 4 * hs)[:, :ff].astype(f32)
    dg_scaled = join(got_gu[:, :, :hs])
    du_scaled = join(got_gu[:, :, hs:])
    grad_w_gate = dg_scaled * gain_two
    grad_w_up = du_scaled * gain_two
    grad_w_down = join(got_down).T

    e_two = both(e_mine, swap(e_mine, "tp")).astype(f32)
    d_middle = grad_out + stat_two * (e_two - scaled_two * jnp.mean(e_two * scaled_two, axis=-1, keepdims=True))
    d_branch = (active * d_middle).astype(bf16)
    d_attended = nn(d_branch, out_t).astype(bf16)
    da4 = d_attended.reshape(seq_len, kv_heads, group, HEAD_SIZE)
    d_probs = jnp.einsum("qhgd,khd->hgqk", da4, v3, preferred_element_type=f32)
    d_value = jnp.einsum("hgqk,qhgd->khd", probs_low, da4, preferred_element_type=f32).reshape(seq_len, kv_cols).astype(bf16)
    d_scores = (probs * (d_probs - jnp.sum(probs * d_probs, axis=-1, keepdims=True))).astype(bf16)
    d_query = jnp.einsum("hgqk,khd->qhgd", d_scores, k3, preferred_element_type=f32).reshape(seq_len, q_cols) * scale
    d_key = jnp.einsum("hgqk,qhgd->khd", d_scores, q4, preferred_element_type=f32).reshape(seq_len, kv_cols) * scale
    d_query = rotate(d_query, cosine, -sine).astype(bf16)
    d_key = rotate(d_key, cosine, -sine).astype(bf16)
    d_qkv = jnp.concatenate([d_query, d_key, d_value], axis=1)
    attn_grad = jnp.concatenate([tn(normed, d_qkv), tn(d_branch, attended)], axis=1).astype(bf16)
    cols = attn_grad.shape[1]
    blocks = attn_grad.reshape(2 * n1, 4, rows, cols).transpose(1, 0, 2, 3)
    got = lax.all_to_all(blocks, ("y", "x"), 0, 0, tiled=True)
    got = jnp.sum(got.astype(f32), axis=0).astype(bf16)
    got = lax.all_to_all(got, ("z1", "z0"), 0, 0, tiled=True)
    owned = jnp.sum(got.astype(f32), axis=0)
    e_part_one = nt(d_qkv, qkv_w)
    e_away = lax.dynamic_slice_in_dim(e_part_one, (1 - core) * half_rows, half_rows, axis=0).astype(bf16)
    e_one = my_half(e_part_one) + swap(e_away, "tp").astype(f32)
    s_one = my_half(scaled_one)
    grad_tokens = (
        my_half(d_middle) + my_half(stat_one) * (e_one - s_one * jnp.mean(e_one * s_one, axis=-1, keepdims=True))
    ).astype(bf16)

    dq_s = owned[:, :q_cols]
    dk_s = owned[:, q_cols : q_cols + kv_cols]
    dv_s = owned[:, q_cols + kv_cols : q_cols + 2 * kv_cols]
    row_sum = lambda w, d: jnp.sum(w.astype(f32) * d, axis=1)
    gain_parts = jnp.stack(
        [
            row_sum(w_query, dq_s) + row_sum(key_matrix, dk_s) + row_sum(value_matrix, dv_s),
            row_sum(w_gate, dg_scaled) + row_sum(w_up, du_scaled),
        ]
    )
    gains = gain_parts + swap(gain_parts, "tp")
    return (
        output,
        grad_tokens,
        dq_s * gain_one,
        dk_s * gain_one,
        dv_s * gain_one,
        owned[:, q_cols + 2 * kv_cols :].T,
        grad_w_gate,
        grad_w_up,
        grad_w_down,
        gains[0],
        gains[1],
    )


def solution(mesh):
    n1 = mesh.shape["fsdp"] // 8
    fine = Mesh(mesh.devices.reshape(n1, 2, 2, 2, mesh.shape["tp"]), ("z1", "z0", "y", "x", "tp"))
    fs = ("z1", "z0", "y", "x")
    both = fs + ("tp",)
    in_specs = (
        P(both, None), P(both, None), P(fs, None), P(fs),
        P(fs, "tp"), P(fs, "tp"), P(fs, "tp"), P("tp", fs),
        P(fs, "tp"), P(fs, "tp"), P("tp", fs), P(fs), P(fs),
    )
    out_specs = (
        P(both, None), P(both, None), P(fs, "tp"), P(fs, "tp"), P(fs, "tp"), P("tp", fs),
        P(fs, "tp"), P(fs, "tp"), P("tp", fs), P(fs), P(fs),
    )
    return jax.shard_map(on_device, mesh=fine, in_specs=in_specs, out_specs=out_specs, check_vma=False)
```

```python
import jax
import jax.numpy as jnp
import numpy as np
from jax import lax
from jax.experimental import pallas as pl
from jax.experimental.pallas import tpu as pltpu
from jax.sharding import Mesh, PartitionSpec as P

HEAD_SIZE = 64
LANES = 128
eps = 1e-05
rotary_base = 10000.0
bf16 = jnp.bfloat16
f32 = jnp.float32
T_AXES = ("z0", "x")
SWAP = [(0, 1), (1, 0)]


def nn(a, b):
    return lax.dot_general(a, b, (((1,), (0,)), ((), ())), preferred_element_type=f32)


def tn(a, b):
    return lax.dot_general(a, b, (((0,), (0,)), ((), ())), preferred_element_type=f32)


def nt(a, b):
    return lax.dot_general(a, b, (((1,), (1,)), ((), ())), preferred_element_type=f32)


def swap(value, axis):
    return lax.ppermute(value, axis, SWAP)


def after(value, *before):
    leaves, tree = jax.tree.flatten(value)
    return jax.tree.unflatten(tree, lax.optimization_barrier(tuple(leaves) + tuple(jax.tree.leaves(before)))[: len(leaves)])


def exchange(blocks, axes):
    return lax.all_to_all(blocks, axes, 0, 0, tiled=True)


def others(value, axes):
    return [lax.ppermute(value, axes, [(i, i ^ k) for i in range(4)]) for k in (1, 2, 3)]


def shape(*dims, dtype=bf16):
    return jax.ShapeDtypeStruct(dims, dtype)


def kernel(body, outs, *args, scalars=None, scratch=()):
    whole = pl.BlockSpec(memory_space=pltpu.VMEM)
    specs = [whole] * len(args)
    if scalars is not None:
        specs = [pl.BlockSpec(memory_space=pltpu.SMEM)] + specs
        args = (scalars,) + args
    return pl.pallas_call(
        body,
        out_shape=list(outs),
        in_specs=specs,
        out_specs=[whole] * len(outs),
        scratch_shapes=list(scratch),
        cost_estimate=pl.CostEstimate(flops=1000, bytes_accessed=1000, transcendentals=0),
        compiler_params=pltpu.CompilerParams(vmem_limit_bytes=60 * 1024 * 1024),
    )(*args)


def join(pieces):
    def body(*refs):
        fill(refs[-1], refs[:-1])

    rows = sum(p.shape[0] for p in pieces)
    return kernel(body, [shape(rows, pieces[0].shape[1])], *pieces)[0]


def gather_line(value):
    if lax.axis_size("z1") == 2:
        return join([value] + others(value, ("z1", "z0")))
    pair = jnp.stack([value, swap(value, "z0")])
    return lax.all_gather(pair, "z1", axis=0).reshape(-1, value.shape[1])


def reduce_y(own, other):
    return (own.astype(f32) + swap(other, "y").astype(f32)).astype(bf16)


def natural_of(n1, rows, letters, relative):
    width = n1 * 8 * rows
    place = lax.broadcasted_iota(jnp.int32, (1, width), 1)
    bits = {}
    rest = place // rows
    for letter in reversed(letters):
        size = n1 if letter == "z1" else 2
        bits[letter] = rest % size
        rest = rest // size
    for letter in letters:
        if letter in relative and (letter != "z1" or n1 == 2):
            bits[letter] = bits[letter] ^ lax.axis_index(letter)
    return (((bits["z1"] * 2 + bits["z0"]) * 2 + bits["y"]) * 2 + bits["x"]) * rows + place % rows


def fill(ref, pieces):
    at = 0
    for p in pieces:
        flat = p[...].reshape(-1, p.shape[-1])
        ref[at : at + flat.shape[0], :] = flat
        at += flat.shape[0]


def column_of(row):
    n = row.shape[1]
    same = lax.broadcasted_iota(jnp.int32, (n, n), 0) == lax.broadcasted_iota(jnp.int32, (n, n), 1)
    return jnp.sum(jnp.where(same, row, 0.0), axis=1, keepdims=True)


def attention_payload(w_query, key_matrix, value_matrix, out_turned, gain):
    rows, q_cols = w_query.shape
    kv = key_matrix.shape[1]

    def body(q, k, v, o, g, out):
        gains = column_of(g[...].astype(f32))
        low = lambda w: w[...].astype(f32) * gains
        out[...] = jnp.concatenate([low(q), low(k), o[...].astype(f32), low(v)], axis=1).astype(bf16)

    return kernel(body, [shape(rows, 2 * q_cols + 2 * kv)], w_query, key_matrix, value_matrix, out_turned, gain)[0]


def feed_forward_payload(w_gate, w_up, down_turned, gain, hs):
    rows, ff = w_gate.shape

    def body(gate, up, down, g, out):
        gains = column_of(g[...].astype(f32))
        blank = jnp.zeros((rows, LANES), bf16)
        per = hs // LANES
        for tile in range(4 * per):
            quarter, place = tile // per, tile % per
            at = tile * LANES
            gate_cols = slice(2 * place * LANES, (2 * place + 1) * LANES)
            up_cols = slice((2 * place + 1) * LANES, (2 * place + 2) * LANES)
            down_cols = slice(2 * hs + place * LANES, 2 * hs + (place + 1) * LANES)
            if at < ff:
                cols = slice(at, at + LANES)
                out[quarter, :, gate_cols] = (gate[:, cols].astype(f32) * gains).astype(bf16)
                out[quarter, :, up_cols] = (up[:, cols].astype(f32) * gains).astype(bf16)
                out[quarter, :, down_cols] = down[:, cols]
            else:
                out[quarter, :, gate_cols] = blank
                out[quarter, :, up_cols] = blank
                out[quarter, :, down_cols] = blank

    return kernel(body, [shape(4, rows, 3 * hs)], w_gate, w_up, down_turned, gain)[0]


def rotary_tables(seq_len):
    half = HEAD_SIZE // 2
    frequency = rotary_base ** (-2.0 * np.arange(half, dtype=np.float32) / HEAD_SIZE)
    angles = np.arange(seq_len, dtype=np.float32)[:, None] * frequency[None, :].astype(np.float32)
    times = 2 * LANES // HEAD_SIZE
    return np.tile(np.cos(angles), (1, times)).astype(np.float32), np.tile(np.sin(angles), (1, times)).astype(np.float32)


def turn(tile, cosine, sine):
    lane = lax.broadcasted_iota(jnp.int32, tile.shape, 1) % HEAD_SIZE
    ahead = pltpu.roll(tile, LANES - HEAD_SIZE // 2, 1)
    behind = pltpu.roll(tile, HEAD_SIZE // 2, 1)
    return tile * cosine + jnp.where(lane < HEAD_SIZE // 2, -ahead, behind) * sine


def upper_half(tile):
    lane = lax.broadcasted_iota(jnp.int32, tile.shape, 1)
    high = jnp.where(lane >= HEAD_SIZE, tile, 0.0)
    return pltpu.roll(high, HEAD_SIZE, 1).astype(bf16), high.astype(bf16)


def softmax_mask(seq_len):
    return lax.broadcasted_iota(jnp.int32, (seq_len, seq_len), 0) >= lax.broadcasted_iota(jnp.int32, (seq_len, seq_len), 1)


def place_halves(ref, core, mine, other):
    half = mine.shape[0]
    ref[pl.ds(pl.multiple_of(core * half, half), half), :] = mine[...].astype(f32)
    ref[pl.ds(pl.multiple_of((1 - core) * half, half), half), :] = other[...].astype(f32)


def attention_forward(scalars, tokens, other_tokens, chunks, order, cosine, sine, heads):
    seq_len, width = 2 * tokens.shape[0], tokens.shape[1]
    cols = chunks[0].shape[1]
    q_wide = heads * HEAD_SIZE + HEAD_SIZE
    tiles = q_wide // LANES
    n_w = len(chunks)
    scale = HEAD_SIZE ** (-0.5)

    def body(*refs):
        s, tok, tok_other, perm, cs, sn = refs[:6]
        w_in = refs[6 : 6 + n_w]
        normed_out, qk_out, v_out, att_out, lse_out, branch_top, branch_low = refs[6 + n_w : 13 + n_w]
        w, whole = refs[13 + n_w :]
        fill(w, w_in)
        place_halves(whole, s[1], tok, tok_other)
        inputs = whole[...]
        stat = lax.rsqrt(jnp.mean(inputs * inputs, axis=-1, keepdims=True) + eps)
        normed = nn((inputs * stat).astype(bf16), perm[...]).astype(bf16)
        normed_out[...] = normed
        cosines, sines = cs[...], sn[...]
        qk = nn(normed, w[:, :q_wide])
        rotated = [turn(qk[:, t * LANES : (t + 1) * LANES], cosines, sines) for t in range(tiles)]
        for t in range(tiles):
            qk_out[:, t * LANES : (t + 1) * LANES] = rotated[t].astype(bf16)
        key_low, key_high = upper_half(rotated[-1])
        value = nn(normed, w[:, cols - LANES :])
        value_low, value_high = upper_half(value)
        v_out[...] = value_high
        seen = softmax_mask(seq_len)
        for t in range(tiles):
            query = rotated[t].astype(bf16)
            total = jnp.zeros((seq_len, LANES), f32)
            for side in (0, 1):
                h = 2 * t + side
                if h >= heads:
                    continue
                scores = jnp.where(seen, nt(query, key_high if side else key_low) * scale, -1e30)
                top = jnp.max(scores, axis=-1, keepdims=True)
                grown = jnp.exp(scores - top)
                mass = jnp.sum(grown, axis=-1, keepdims=True)
                lse_out[:, h : h + 1] = top + jnp.log(mass)
                probs = (grown / mass).astype(bf16)
                total = total + nn(probs, value_high if side else value_low)
            att_out[:, t * LANES : (t + 1) * LANES] = total.astype(bf16)
        branch = nt(att_out[...], w[:, q_wide:]).astype(bf16)
        branch = nt(branch, perm[...]).astype(bf16)
        branch_top[...] = branch[: seq_len // 2]
        branch_low[...] = branch[seq_len // 2 :]

    return kernel(
        body,
        [
            shape(seq_len, width), shape(seq_len, q_wide), shape(seq_len, LANES), shape(seq_len, q_wide),
            shape(seq_len, LANES, dtype=f32), shape(seq_len // 2, width), shape(seq_len // 2, width),
        ],
        tokens, other_tokens, order, cosine, sine, *chunks,
        scalars=scalars,
        scratch=[pltpu.VMEM((width, cols), bf16), pltpu.VMEM((seq_len, width), f32)],
    )


def middle_step(scalars, tokens, other_tokens, branches, order):
    half, width = tokens.shape
    seq_len = 2 * half

    def body(s, tok, tok_other, top, low, top_other, low_other, perm, middle_out, x_out):
        active = s[0].astype(f32)
        place_halves(middle_out, s[1], tok, tok_other)
        for rows, a, b in ((slice(0, half), top, top_other), (slice(half, seq_len), low, low_other)):
            middle_out[rows, :] = middle_out[rows, :] + active * (a[...].astype(f32) + b[...].astype(f32))
        at = pl.multiple_of(s[1] * half, half)
        own = middle_out[pl.ds(at, half), :]
        stat = lax.rsqrt(jnp.mean(own * own, axis=-1, keepdims=True) + eps)
        x = nn((own * stat).astype(bf16), perm[...]).astype(bf16)
        for t in range(4):
            x_out[t, :, :] = x

    return kernel(body, [shape(seq_len, width, dtype=f32), shape(4, half, width)], tokens, other_tokens, *branches, order, scalars=scalars)


def cotangent_step(scalars, cotangent, order):
    half, width = cotangent.shape

    def body(s, cot, perm, out):
        c = nn((s[0].astype(f32) * cot[...].astype(f32)).astype(bf16), perm[...]).astype(bf16)
        for t in range(4):
            out[t, :, :] = c

    return kernel(body, [shape(4, half, width)], cotangent, order, scalars=scalars)[0]


def hidden_units(xs, gus):
    n_x, n_w = len(xs), len(gus)
    tokens = sum(x.shape[0] * x.shape[1] for x in xs)
    width = xs[0].shape[-1]
    hs = gus[0].shape[1] // 2

    def body(*refs):
        x_in, w_in = refs[:n_x], refs[n_x : n_x + n_w]
        hid, slope, x, w = refs[n_x + n_w :]
        fill(x, x_in)
        fill(w, w_in)

        def block(i, carry):
            at = pl.multiple_of(i * LANES, LANES)
            at2 = pl.multiple_of(i * 2 * LANES, 2 * LANES)
            gu = nn(x[...], w[:, pl.ds(at2, 2 * LANES)])
            gate, up = gu[:, :LANES], gu[:, LANES:]
            sig = 1.0 / (1.0 + jnp.exp(-gate))
            act = gate * sig
            hid[:, pl.ds(at, LANES)] = (act * up).astype(bf16)
            slope[:, pl.ds(at2, LANES)] = (up * sig * (1.0 + gate * (1.0 - sig))).astype(bf16)
            slope[:, pl.ds(pl.multiple_of(at2 + LANES, LANES), LANES)] = act.astype(bf16)
            return carry

        lax.fori_loop(0, hs // LANES, block, 0)

    return kernel(
        body,
        [shape(tokens, hs), shape(tokens, 2 * hs)],
        *xs, *gus,
        scratch=[pltpu.VMEM((tokens, width), bf16), pltpu.VMEM((width, 2 * hs), bf16)],
    )


def hidden_back(cs, slope, gus, downs):
    n_x, n_w = len(cs), len(gus)
    tokens = slope.shape[0]
    half = tokens // 2
    width = cs[0].shape[-1]
    hs = downs[0].shape[1]

    def body(*refs):
        c_in, slope_r = refs[:n_x], refs[n_x]
        g_in, d_in = refs[n_x + 1 : n_x + 1 + n_w], refs[n_x + 1 + n_w : n_x + 1 + 2 * n_w]
        e_mine, e_away, dgu, c, wg, wd = refs[n_x + 1 + 2 * n_w :]
        fill(c, c_in)
        fill(wd, d_in)
        fill(wg, g_in)

        def block(i, carry):
            at = pl.multiple_of(i * LANES, LANES)
            at2 = pl.multiple_of(i * 2 * LANES, 2 * LANES)
            at3 = pl.multiple_of(at2 + LANES, LANES)
            dh = nn(c[...], wd[:, pl.ds(at, LANES)])
            dgu[:, pl.ds(at2, LANES)] = (dh * slope_r[:, pl.ds(at2, LANES)].astype(f32)).astype(bf16)
            dgu[:, pl.ds(at3, LANES)] = (dh * slope_r[:, pl.ds(at3, LANES)].astype(f32)).astype(bf16)
            return carry

        lax.fori_loop(0, hs // LANES, block, 0)

        def rows_of(out, base):
            for q in range(half // 256):
                piece = nt(dgu[base + q * 256 : base + (q + 1) * 256, :], wg[...]).astype(bf16)
                out[2 * q, :, :] = piece[:128]
                out[2 * q + 1, :, :] = piece[128:]

        rows_of(e_away, half)
        rows_of(e_mine, 0)

    quads = shape(4, half // 4, width)
    return kernel(
        body,
        [quads, quads, shape(tokens, 2 * hs)],
        *cs, slope, *gus, *downs,
        scratch=[pltpu.VMEM((tokens, width), bf16), pltpu.VMEM((width, 2 * hs), bf16), pltpu.VMEM((width, hs), bf16)],
    )


def weight_grads(lefts, right, parts):
    n_x = len(lefts)
    tokens, cols = right.shape
    width = lefts[0].shape[-1]
    h = width // 2
    each = cols // parts

    def body(*refs):
        right_r, outs, x = refs[n_x], refs[n_x + 1 : n_x + 1 + 2 * parts], refs[n_x + 1 + 2 * parts]
        fill(x, refs[:n_x])

        def step(i, carry):
            at = pl.multiple_of(i * LANES, LANES)
            for p in range(parts):
                whole = tn(x[...], right_r[:, pl.ds(pl.multiple_of((i * parts + p) * LANES, LANES), LANES)]).astype(bf16)
                outs[2 * p][:, pl.ds(at, LANES)] = whole[:h]
                outs[2 * p + 1][:, pl.ds(at, LANES)] = whole[h:]
            return carry

        lax.fori_loop(0, each // LANES, step, 0)

    return kernel(body, [shape(h, each)] * (2 * parts), *lefts, right, scratch=[pltpu.VMEM((tokens, width), bf16)])


def ff_output(hid, downs):
    tokens, hs = hid.shape
    n_w = len(downs)
    width = sum(d.shape[0] for d in downs)
    half = tokens // 2

    def body(*refs):
        hid_r, d_in = refs[0], refs[1 : 1 + n_w]
        mine, away, wd = refs[1 + n_w :]
        fill(wd, d_in)
        for out, base in ((away, half), (mine, 0)):
            for q in range(half // 256):
                piece = nt(hid_r[base + q * 256 : base + (q + 1) * 256, :], wd[...]).astype(bf16)
                out[2 * q, :, :] = piece[:128]
                out[2 * q + 1, :, :] = piece[128:]

    quads = shape(4, half // 4, width)
    return kernel(body, [quads, quads], hid, *downs, scratch=[pltpu.VMEM((width, hs), bf16)])


def add_pair(mine, other):
    return (mine.astype(f32) + other.astype(f32)).astype(bf16)


def sum_natural(parts, order):
    _, rows, width = parts.shape

    def body(p, perm, out):
        total = p[0].astype(f32) + p[1].astype(f32) + p[2].astype(f32) + p[3].astype(f32)
        out[...] = nt(total.astype(bf16), perm[...]).astype(bf16)

    return kernel(body, [shape(rows, width)], parts, order)[0]


def output_step(scalars, parts, order, middle):
    _, rows, width = parts.shape

    def body(s, p, perm, mid, out):
        total = p[0].astype(f32) + p[1].astype(f32) + p[2].astype(f32) + p[3].astype(f32)
        own = mid[pl.ds(pl.multiple_of(s[1] * rows, rows), rows), :]
        out[...] = (own + s[0].astype(f32) * nt(total.astype(bf16), perm[...])).astype(bf16)

    return kernel(body, [shape(rows, width)], parts, order, middle, scalars=scalars)[0]


def attention_backward(scalars, e_mine, e_other, cot, other_cot, middle, order, cosine, sine, normed, qk, value, attended, lse, chunks, heads):
    seq_len, width = middle.shape
    half = seq_len // 2
    cols = chunks[0].shape[1]
    q_wide = heads * HEAD_SIZE + HEAD_SIZE
    tiles = q_wide // LANES
    n_w = len(chunks)
    scale = HEAD_SIZE ** (-0.5)

    def body(*refs):
        s, em, eo, co, co_other, mid, perm, cs, sn, nrm, qk_r, v_r, att, lse_r = refs[:14]
        w_in = refs[14 : 14 + n_w]
        dw_outs = refs[14 + n_w : 18 + n_w]
        e_keep, e_away, dmid_out = refs[18 + n_w : 21 + n_w]
        w, e_all, dqk, whole_e = refs[21 + n_w :]
        fill(w, w_in)
        core = s[1]
        active = s[0].astype(f32)
        mine_at = pl.multiple_of(core * half, half)
        other_at = pl.multiple_of((1 - core) * half, half)
        place_halves(e_all, core, em, eo)
        place_halves(whole_e, core, co, co_other)
        middles = mid[...]
        stat = lax.rsqrt(jnp.mean(middles * middles, axis=-1, keepdims=True) + eps)
        scaled = middles * stat
        e = e_all[...]
        d_middle = whole_e[...] + stat * (e - scaled * jnp.mean(e * scaled, axis=-1, keepdims=True))
        e_all[...] = d_middle
        dmid_out[...] = e_all[pl.ds(mine_at, half), :]
        d_branch = nn((active * d_middle).astype(bf16), perm[...]).astype(bf16)
        d_att = nn(d_branch, w[:, q_wide:]).astype(bf16)
        key_low, key_high = upper_half(qk_r[:, q_wide - LANES :].astype(f32))
        value_low, value_high = upper_half(v_r[...].astype(f32))
        seen = softmax_mask(seq_len)
        d_key = [jnp.zeros((seq_len, LANES), f32), jnp.zeros((seq_len, LANES), f32)]
        d_value = [jnp.zeros((seq_len, LANES), f32), jnp.zeros((seq_len, LANES), f32)]
        cosines, sines = cs[...], -sn[...]
        last = None
        for t in range(tiles):
            query = qk_r[:, t * LANES : (t + 1) * LANES]
            da = d_att[:, t * LANES : (t + 1) * LANES]
            total = jnp.zeros((seq_len, LANES), f32)
            for side in (0, 1):
                h = 2 * t + side
                if h >= heads:
                    continue
                key = key_high if side else key_low
                scores = jnp.where(seen, nt(query, key) * scale, -1e30)
                probs = jnp.exp(scores - lse_r[:, h : h + 1])
                d_probs = nt(da, value_high if side else value_low)
                d_value[side] = d_value[side] + tn(probs.astype(bf16), da)
                d_scores = (probs * (d_probs - jnp.sum(probs * d_probs, axis=-1, keepdims=True))).astype(bf16)
                total = total + nn(d_scores, key)
                d_key[side] = d_key[side] + tn(d_scores, query)
            if t < tiles - 1:
                dqk[:, t * LANES : (t + 1) * LANES] = turn(total * scale, cosines, sines).astype(bf16)
            else:
                last = total
        lane = lax.broadcasted_iota(jnp.int32, (seq_len, LANES), 1)
        low_lane = lane < HEAD_SIZE
        key_total = jnp.where(low_lane, last, d_key[1] + pltpu.roll(d_key[0], HEAD_SIZE, 1))
        dqk[:, q_wide - LANES :] = turn(key_total * scale, cosines, sines).astype(bf16)
        dv = jnp.where(low_lane, 0.0, d_value[1] + pltpu.roll(d_value[0], HEAD_SIZE, 1)).astype(bf16)
        normed_t = nrm[...]
        d_all = dqk[...]
        first = tn(normed_t, d_all)
        second = tn(d_branch, att[...])
        third = tn(normed_t, dv)
        quarter = width // 4
        for q in range(4):
            rows = slice(q * quarter, (q + 1) * quarter)
            dw_outs[q][:, :q_wide] = first[rows].astype(bf16)
            dw_outs[q][:, q_wide : cols - LANES] = second[rows, : q_wide - LANES].astype(bf16)
            dw_outs[q][:, cols - LANES :] = (second[rows, q_wide - LANES :] + third[rows]).astype(bf16)
        e_one = (nt(d_all, w[:, :q_wide]) + nt(dv, w[:, cols - LANES :])).astype(bf16)
        whole_e[...] = nt(e_one, perm[...])
        e_keep[...] = whole_e[pl.ds(mine_at, half), :]
        e_away[...] = whole_e[pl.ds(other_at, half), :].astype(bf16)

    return kernel(
        body,
        [shape(width // 4, cols)] * 4 + [shape(half, width, dtype=f32), shape(half, width), shape(half, width, dtype=f32)],
        e_mine, e_other, cot, other_cot, middle, order, cosine, sine, normed, qk, value, attended, lse, *chunks,
        scalars=scalars,
        scratch=[
            pltpu.VMEM((width, cols), bf16), pltpu.VMEM((seq_len, width), f32),
            pltpu.VMEM((seq_len, q_wide), bf16), pltpu.VMEM((seq_len, width), f32),
        ],
    )


def tokens_step(tokens, e_keep, e_other, d_middle):
    def body(tok, keep, other, dm, out):
        inputs = tok[...].astype(f32)
        stat = lax.rsqrt(jnp.mean(inputs * inputs, axis=-1, keepdims=True) + eps)
        scaled = inputs * stat
        e = keep[...] + other[...].astype(f32)
        out[...] = (dm[...] + stat * (e - scaled * jnp.mean(e * scaled, axis=-1, keepdims=True))).astype(bf16)

    return kernel(body, [shape(*tokens.shape)], tokens, e_keep, e_other, d_middle)[0]


def on_device(
    tokens, cotangent, parents, skip, w_query, key_matrix, value_matrix, w_out, w_gate, w_up, w_down, gain_attn, gain_mlp
):
    half_rows, width = tokens.shape
    seq_len = 2 * half_rows
    rows = w_query.shape[0]
    n1 = lax.axis_size("z1")
    q_cols = w_query.shape[1]
    kv_cols = key_matrix.shape[1]
    heads = q_cols // HEAD_SIZE
    ff = w_gate.shape[1]
    hs = -(-ff // (4 * LANES)) * LANES
    core = lax.axis_index("tp")
    scalars = jnp.stack([1 - skip[0], core.astype(jnp.int32)])
    cos_np, sin_np = rotary_tables(seq_len)
    cosine, sine = jnp.asarray(cos_np), jnp.asarray(sin_np)
    gain_one = gain_attn.astype(f32)[:, None]
    gain_two = gain_mlp.astype(f32)[:, None]

    attn_own = attention_payload(w_query, key_matrix, value_matrix, w_out.T, gain_attn[None, :])
    ff_in = after((w_gate, w_up, w_down.T), attn_own)
    ff_blocks = feed_forward_payload(*ff_in, gain_mlp[None, :], hs)
    other_tokens = swap(tokens, "tp")
    other_cot = swap(cotangent, "tp")
    natural = lax.broadcasted_iota(jnp.int32, (width, 1), 0)
    to_hidden = (natural == natural_of(n1, rows, ("y", "z1", "z0", "x"), ("y", "z1"))).astype(bf16)
    to_attn = (natural == natural_of(n1, rows, ("y", "x", "z1", "z0"), ("y", "x", "z1", "z0"))).astype(bf16)
    c_wide = cotangent_step(scalars, cotangent, to_hidden)
    attn_line = after(gather_line(attn_own), to_hidden, to_attn, c_wide, other_tokens, other_cot)
    ff_t = exchange(ff_blocks, T_AXES).reshape(4 * rows, 3 * hs)
    gu_t, down_t = ff_t[:, : 2 * hs], ff_t[:, 2 * hs :]

    line_y = swap(attn_line, "y")
    attn_w = [attn_line, swap(attn_line, "x"), line_y, swap(line_y, "x")]
    two = n1 == 2
    if two:
        gu_z, gu_y = swap(gu_t, "z1"), swap(gu_t, "y")
        other_tokens, c_wide = after((other_tokens, c_wide), attn_w, gu_z, gu_y)

    own_c = exchange(c_wide, T_AXES)
    normed, qk, value, attended, lse, *branch = attention_forward(scalars, tokens, other_tokens, attn_w, to_attn, cosine, sine, heads)
    branch = branch + [swap(b, "tp") for b in branch]
    if two:
        gu_zy, down_z = swap(gu_z, "y"), swap(down_t, "z1")
        branch = after(branch, gu_zy, down_z, own_c)
    middle, x_wide = middle_step(scalars, tokens, other_tokens, branch, to_hidden)
    own_x = exchange(x_wide, T_AXES)
    if two:
        down_y, down_zy = swap(after(down_t, x_wide), "y"), swap(after(down_z, x_wide), "y")
        own_x = after(own_x, down_y, down_zy)
        gus = [gu_t, gu_z, gu_y, gu_zy]
        downs = [down_t, down_z, down_y, down_zy]
    else:
        gu_all, down_all = (lax.all_gather(v, "z1", axis=0, tiled=True) for v in (gu_t, down_t))
        gus, downs = [gu_all, swap(gu_all, "y")], [down_all, swap(down_all, "y")]
    xs = [own_x, swap(own_x, "tp")]
    cs = [own_c, swap(after(own_c, x_wide), "tp")]

    hidden, slope = hidden_units(xs, gus)
    d_own, d_other = weight_grads(cs, hidden, 1)
    e_keep, e_away, d_gu = hidden_back(cs, after(slope, d_other), gus, downs)
    e_sum = add_pair(e_keep, swap(e_away, "tp"))
    e_parts = exchange(e_sum, T_AXES)
    gate_own, gate_other, up_own, up_other = weight_grads(xs, after(d_gu, e_sum), 2)
    m_keep, m_away = ff_output(after(hidden, up_other), downs)
    e_mine = sum_natural(after(e_parts, m_keep), to_hidden)
    m_sum = add_pair(m_keep, swap(m_away, "tp"))
    m_parts = exchange(after(m_sum, e_mine), T_AXES)
    half_down = reduce_y(d_own, d_other)
    e_mine = after(e_mine, half_down)

    dw_parts = attention_backward(
        scalars, e_mine, swap(e_mine, "tp"), cotangent, other_cot, middle, to_attn, cosine, sine, normed, qk, value, attended, lse, attn_w, heads
    )
    e1_keep, e1_away, d_middle = dw_parts[4:]
    far = (dw_parts[2].astype(f32) + swap(dw_parts[3], "x").astype(f32)).astype(bf16)
    line_sum = dw_parts[0].astype(f32) + swap(dw_parts[1], "x").astype(f32) + swap(far, "y").astype(f32)
    line_sum = line_sum.astype(bf16)
    output = output_step(scalars, after(m_parts, line_sum), to_hidden, middle)

    halves = [half_down, reduce_y(after(gate_own, dw_parts), gate_other), reduce_y(after(up_own, dw_parts), up_other)]
    if two:
        mine = [h[: 4 * rows] for h in halves]
        from_z = after([swap(h[4 * rows :], "z1") for h in halves], line_sum)
        summed = [(a.astype(f32) + b.astype(f32)).astype(bf16) for a, b in zip(mine, from_z)]
    else:
        summed = [
            jnp.sum(exchange(h.reshape(n1, 4 * rows, hs), "z1").astype(f32), axis=0).astype(bf16) for h in halves
        ]
    got_ff = exchange(after(jnp.concatenate(summed, axis=1).reshape(4, rows, 3 * hs), m_parts), T_AXES)
    if two:
        parts = line_sum.reshape(4, rows, -1)
        owned = parts[0].astype(f32)
        for k in (1, 2, 3):
            owned = owned + lax.ppermute(parts[k], ("z1", "z0"), [(i, i ^ k) for i in range(4)]).astype(f32)
    else:
        got = jnp.sum(exchange(line_sum.reshape(n1, 2, rows, -1), "z1").astype(f32), axis=0)
        owned = got[0] + swap(got[1].astype(bf16), "z0").astype(f32)
    grad_tokens = tokens_step(tokens, e1_keep, swap(e1_away, "tp"), d_middle)

    whole = lambda got: got.astype(f32).transpose(1, 0, 2).reshape(rows, 4 * hs)[:, :ff]
    down_s, dg_scaled, du_scaled = (whole(got_ff[:, :, k * hs : (k + 1) * hs]) for k in range(3))
    grad_w_down = down_s.T

    dq_s = owned[:, :q_cols]
    dk_s = owned[:, q_cols : q_cols + kv_cols]
    d_out = owned[:, q_cols + kv_cols : 2 * q_cols + kv_cols]
    dv_s = owned[:, 2 * q_cols + kv_cols :]
    row_sum = lambda w, d: jnp.sum(w.astype(f32) * d, axis=1)
    gain_parts = jnp.stack(
        [
            row_sum(w_query, dq_s) + row_sum(key_matrix, dk_s) + row_sum(value_matrix, dv_s),
            row_sum(w_gate, dg_scaled) + row_sum(w_up, du_scaled),
        ]
    )
    gains = gain_parts + swap(gain_parts, "tp")
    return (
        output,
        grad_tokens,
        dq_s * gain_one,
        dk_s * gain_one,
        dv_s * gain_one,
        d_out.T,
        dg_scaled * gain_two,
        du_scaled * gain_two,
        grad_w_down,
        gains[0],
        gains[1],
    )


def solution(mesh):
    n1 = mesh.shape["fsdp"] // 8
    fine = Mesh(mesh.devices.reshape(n1, 2, 2, 2, mesh.shape["tp"]), ("z1", "z0", "y", "x", "tp"))
    fs = ("z1", "z0", "y", "x")
    both = fs + ("tp",)
    in_specs = (
        P(both, None), P(both, None), P(fs, None), P(fs),
        P(fs, "tp"), P(fs, "tp"), P(fs, "tp"), P("tp", fs),
        P(fs, "tp"), P(fs, "tp"), P("tp", fs), P(fs), P(fs),
    )
    out_specs = (
        P(both, None), P(both, None), P(fs, "tp"), P(fs, "tp"), P(fs, "tp"), P("tp", fs),
        P(fs, "tp"), P(fs, "tp"), P("tp", fs), P(fs), P(fs),
    )
    return jax.shard_map(on_device, mesh=fine, in_specs=in_specs, out_specs=out_specs, check_vma=False)
```
